32 devices in a mesh: row: 8 (over y, x, core), ck: 4 (over z).
Axes of the slice: x: 2, y: 2, z: 4, core: 2. Of those that a mesh axis runs over, the one named last changes fastest.
Arguments:
- amp_tiles: bfloat16 [8, 4, 8, 16, 128, 128], P('row', 'ck'), may hold values from -6 to 6
- tile_pos: int32 [8, 4, 8, 16], P(None, 'ck'), may hold values from 0 to 2303, as said below
- tile_count: int32 [8, 4, 8], P(None, 'ck'), may hold values from 0 to 16, as said below
- cycle_integrals: bfloat16 [147456, 512], P('ck'), may hold values from -0.09375 to 0.09375
- row_gap: float32 [8192], P(('row', 'ck')), may hold values from 0.5 to 4
- col_gap: float32 [512], replicated, may hold values from 0.5 to 4
Outputs:
- new_amp: bfloat16 [8192, 512], P(('row', 'ck'))
The draws below stay inside these ranges and needn't reach their ends.
Inputs may be any that keep to these rules, and one draw needn't show every extreme that they name: `tile_pos`: slots 0 to tile_count - 1 of each list are live, the others hold no tile. Within one ck group and one row owner all slots' positions are distinct. `tile_count`: in every ck group one row owner receives 16 live tiles from every storage owner.
All inputs are finite; a program needn't handle non-finite values.
Results may differ from the reference program's by a relative error of at most 0.001.
Values may be sent and summed in bfloat16 or wider, within the bound.
No kernel may reach another device: no remote copies, remote signals or barrier semaphores. Data moves between devices by JAX's collectives and lax.ppermute only.
A program may use at most 320 MiB of HBM per device.

```python
import math
import jax
import jax.numpy as jnp
from jax import lax

TILE = 128
KT_DEV = 288
ROWT_DEV = 8
CAP = 16
COLS = 512
OWNERS = 8
GROUPS = 4
ROWS = 8192
CKROWS = 147456
N_ROW = 8
N_CK = 4


def tile_pattern(key):
    base_key = jax.random.fold_in(key, 7)
    place_key, count_key, full_key = jax.random.split(base_key, 3)
    total = ROWT_DEV * KT_DEV
    slot_total = OWNERS * CAP

    def one_list(sub_key):
        first_key, second_key = jax.random.split(sub_key)
        middle = (jax.random.permutation(first_key, total - 2) + 1).astype(jnp.int32)
        ordered = jnp.concatenate([jnp.array([0, total - 1], jnp.int32), middle])[:slot_total]
        return jax.random.permutation(second_key, ordered).astype(jnp.int32)
    list_keys = jax.random.split(place_key, GROUPS * OWNERS)
    lists = jax.vmap(one_list)(list_keys).reshape(GROUPS, OWNERS, OWNERS, CAP)
    positions = jnp.transpose(lists, (2, 0, 1, 3)).astype(jnp.int32)
    counts = jax.random.randint(count_key, (OWNERS, GROUPS, OWNERS), 0, CAP + 1)
    full_owner = jax.random.randint(full_key, (GROUPS,), 0, OWNERS)
    is_full = jnp.arange(OWNERS)[None, :] == full_owner[:, None]
    counts = jnp.where(is_full[None, :, :], CAP, counts).astype(jnp.int32)
    return (positions, counts)


def draw_tile_pos(key, part):
    return tile_pattern(key)[0]


def draw_tile_count(key, part):
    return tile_pattern(key)[1]


def block_levels(stream_key, dims, shards, least, top_value):
    factor_of, own = 1.0, jax.random.fold_in(stream_key, 6)
    for axis_at, parts in shards:
        draws = jnp.exp(jax.random.uniform(jax.random.fold_in(own, axis_at), (parts,), jnp.float32, least / len(shards), top_value / len(shards)))
        factor_of = factor_of * jnp.repeat(draws, dims[axis_at] // parts).reshape([-1 if axis == axis_at else 1 for axis in range(len(dims))])
    return factor_of


def normal_values(own_key, extent, deviation, reach, pieces=(), held_as=jnp.bfloat16):
    entries = jax.random.normal(own_key, extent, jnp.float32) * deviation
    if len(pieces) > 0:
        entries = block_levels(own_key, extent, pieces, -0.22, 0.18) * entries
    return jnp.clip(entries, min=-reach, max=reach).astype(held_as)


def setup_inputs(seed: int = 0) -> dict:
    splits = jax.random.split(jax.random.key(seed), 7)
    return {
        "amp_tiles": normal_values(splits[0], (OWNERS, GROUPS, OWNERS, CAP, TILE, TILE), 1.0, 6.0, ((0, 8), (1, 4))),
        "tile_pos": draw_tile_pos(jax.random.fold_in(splits[6], 71), 0),
        "tile_count": draw_tile_count(jax.random.fold_in(splits[6], 71), 0),
        "cycle_integrals": normal_values(splits[3], (CKROWS, COLS), (TILE * N_CK * CAP * N_ROW // (2 * ROWT_DEV)) ** -0.5, 0.09375, ((0, 4),)),
        "row_gap": jnp.clip(jnp.exp(math.log(4.0) - 2.0794415 * jax.random.uniform(splits[4], (ROWS,), jnp.float32) ** block_levels(splits[4], (ROWS,), ((0, 32),), -0.2, 0.2)), 0.5, 4.0),
        "col_gap": jnp.clip(jnp.exp(jax.random.uniform(splits[5], (COLS,), jnp.float32, math.log(0.5), math.log(4.0))), 0.5, 4.0),
    }


def reference(amp_tiles, tile_pos, tile_count, cycle_integrals, row_gap, col_gap):
    blocks = cycle_integrals.reshape(N_CK, KT_DEV, TILE, COLS)
    slot_range = jnp.arange(CAP, dtype=jnp.int32)
    tile_range = jnp.arange(ROWT_DEV, dtype=jnp.int32)

    def add_pair(totals, pair_index):
        group_index = pair_index // N_ROW
        owner_index = pair_index % N_ROW
        in_group = lax.dynamic_index_in_dim(amp_tiles, group_index, 1, keepdims=False)
        amp_slots = lax.dynamic_index_in_dim(in_group, owner_index, 1, keepdims=False).reshape(N_ROW * CAP, TILE, TILE)
        pos_group = lax.dynamic_index_in_dim(tile_pos, group_index, 1, keepdims=False)
        positions = lax.dynamic_index_in_dim(pos_group, owner_index, 1, keepdims=False).reshape(-1)
        count_group = lax.dynamic_index_in_dim(tile_count, group_index, 1, keepdims=False)
        counts = lax.dynamic_index_in_dim(count_group, owner_index, 1, keepdims=False).reshape(-1)
        live_mask = (slot_range[None, :] < counts[:, None]).reshape(-1)
        group_blocks = lax.dynamic_index_in_dim(blocks, group_index, 0, keepdims=False)
        picked = group_blocks[positions % KT_DEV]
        products = jnp.einsum("mrk,mkc->mrc", amp_slots.astype(jnp.float32), picked.astype(jnp.float32), precision=lax.Precision.HIGHEST)
        selector = ((positions // KT_DEV)[None, :] == tile_range[:, None]) & live_mask[None, :]
        summed = jnp.einsum("im,mrc->irc", selector.astype(jnp.float32), products, precision=lax.Precision.HIGHEST)
        summed = summed.reshape(ROWT_DEV * TILE, COLS)
        row_start = (owner_index * (ROWT_DEV * TILE)).astype(jnp.int32)
        current = lax.dynamic_slice_in_dim(totals, row_start, ROWT_DEV * TILE, 0)
        return lax.dynamic_update_slice_in_dim(totals, current + summed, row_start, 0), None

    initial = jnp.zeros((ROWS, COLS), jnp.float32)
    totals = lax.scan(add_pair, initial, jnp.arange(N_CK * N_ROW, dtype=jnp.int32))[0]
    update = (totals / (row_gap[:, None] + col_gap[None, :])).astype(jnp.bfloat16)
    piece_rows = ROWT_DEV * TILE // (N_CK * N_ROW)
    reordered = update.reshape(N_ROW, N_CK, N_ROW, piece_rows, COLS).transpose(2, 1, 0, 3, 4)
    return reordered.reshape(ROWS, COLS)
```

```python
import functools
import jax
import jax.numpy as jnp
from jax import lax
from jax.experimental import pallas as pl
from jax.experimental.pallas import tpu as pltpu
from jax.sharding import PartitionSpec as P

SUB = 8
UNROLL = 4
QMAX = 32000.0
SHARES = (2, 2)
AHEAD = 2
ANY = pl.BlockSpec(memory_space=pl.ANY)
HBM = pl.BlockSpec(memory_space=pltpu.HBM)
SMEM = pl.BlockSpec(memory_space=pltpu.SMEM)
VM = pl.BlockSpec(memory_space=pltpu.VMEM)


def pack_kernel(n_row, first, units, amp, after, *refs):
    outs, (buf, sem_in, sem_out) = refs[:-3], refs[-3:]
    me = lax.axis_index("row")
    ins, puts = [], []
    for k in range(n_row):
        o = jnp.bitwise_xor(me, k)
        ins.append(pltpu.make_async_copy(amp.at[o, :, :, pl.ds(first, units)], buf.at[k], sem_in.at[k]))
        puts.append(pltpu.make_async_copy(buf.at[k], outs[k], sem_out.at[k]))
    for x in ins:
        x.start()
    for x, y in zip(ins, puts):
        x.wait()
        y.start()
    for y in puts:
        y.wait()


def pack(amp, first, units, after):
    n_row, cap, q, _, sub, tile = amp.shape
    shape = (cap, q, units, sub, tile)
    outs = pl.pallas_call(
        functools.partial(pack_kernel, n_row, first, units),
        out_shape=[jax.ShapeDtypeStruct(shape, amp.dtype)] * n_row,
        in_specs=[HBM, ANY], out_specs=[ANY] * n_row,
        scratch_shapes=[pltpu.VMEM((n_row,) + shape, amp.dtype), pltpu.SemaphoreType.DMA((n_row,)), pltpu.SemaphoreType.DMA((n_row,))],
        cost_estimate=pl.CostEstimate(flops=0, bytes_accessed=4 * n_row * cap * q * units * sub * tile, transcendentals=0),
        compiler_params=pltpu.CompilerParams(vmem_limit_bytes=16 << 20),
        name="pack",
    )(amp, after)
    return [x.reshape(cap, q * units * sub, tile) for x in outs]


def plan_kernel(n_row, cap, kt, pos, cnt, w, lists, wsort, off, sem):
    me = lax.axis_index("row")
    rowt = off.shape[0] // 2
    slots = n_row * cap
    most = (lists.shape[0] - 1) // 4

    def each(fn):
        def outer(k, carry):
            s = jnp.bitwise_xor(me, k)

            def inner(m, carry):
                fn(k * cap + m, pos[s, 0, me, m])
                return carry

            return lax.fori_loop(0, cnt[s, 0, me], inner, carry)

        lax.fori_loop(0, n_row, outer, 0)

    for t in range(rowt):
        off[rowt + t] = 0

    def count(slot, p):
        t = p // kt
        off[rowt + t] += 1

    each(count)
    at = jnp.int32(0)
    for t in range(rowt):
        off[t] = at
        pairs = (off[rowt + t] + 1) // 2

        def mark(j, base):
            lists[3 * most + base + j] = t
            lists[2 * most + base + j] = base + j
            return base

        lax.fori_loop(0, pairs, mark, at // 2)
        at += 2 * pairs

    def put(i, slot, block):
        lists[lax.rem(i, 2) * most + i // 2] = slot
        pltpu.make_async_copy(w.at[block], wsort.at[i], sem).start()

    def place(slot, p):
        t = p // kt
        i = off[t]
        off[t] = i + 1
        put(i, slot, p - t * kt)

    each(place)
    for t in range(rowt):
        @pl.when(lax.rem(off[rowt + t], 2) == 1)
        def _():
            put(off[t], slots, 0)
    pairs = at // 2

    def fill(j, _):
        lists[j] = slots
        lists[most + j] = slots
        lists[2 * most + j] = 0
        lists[3 * most + j] = 0
        return _

    whole = (pairs + UNROLL - 1) // UNROLL
    lax.fori_loop(pairs, whole * UNROLL, fill, 0)
    lists[4 * most] = whole

    def wait(i, _):
        pltpu.make_async_copy(w.at[0], wsort.at[i], sem).wait()
        return _

    lax.fori_loop(0, at, wait, 0)


def plan(pos, cnt, w, rowt):
    n_row, _, _, cap = pos.shape
    kt, tile, cols = w.shape
    held = n_row * cap + rowt
    most = held // 2 + UNROLL
    return pl.pallas_call(
        functools.partial(plan_kernel, n_row, cap, kt),
        out_shape=[jax.ShapeDtypeStruct((4 * most + 1,), jnp.int32), pltpu.VMEM((held, tile, cols), w.dtype)],
        in_specs=[SMEM, SMEM, HBM],
        out_specs=[SMEM, VM],
        scratch_shapes=[pltpu.SMEM((2 * rowt,), jnp.int32), pltpu.SemaphoreType.DMA],
        cost_estimate=pl.CostEstimate(flops=0, bytes_accessed=held * tile * cols * 2, transcendentals=0),
        compiler_params=pltpu.CompilerParams(vmem_limit_bytes=4 << 20),
        name="plan",
    )(pos, cnt, w)


def contract_kernel(n_row, n_ck, lists, wsort, *refs):
    pieces, own, outs = refs[:n_row], refs[n_row], refs[n_row + 1:n_row + n_ck]
    amp, acc, asem = refs[n_row + n_ck:]
    mine = lax.axis_index("ck")
    cap, width, tile = pieces[0].shape
    slots = n_row * cap
    cols = acc.shape[1]
    most = (lists.shape[0] - 1) // 4
    loads = [pltpu.make_async_copy(pieces[k], amp.at[pl.ds(k * cap, cap)], asem.at[k]) for k in range(n_row)]
    for x in loads:
        x.start()
    acc[...] = jnp.zeros_like(acc)
    amp[slots] = jnp.zeros((width, tile), amp.dtype)
    for x in loads:
        x.wait()

    def group(g, _):
        js = [g * UNROLL + u for u in range(UNROLL)]
        ps = []
        for j in js:
            a = jnp.concatenate([amp[lists[j]], amp[lists[most + j]]], axis=1)
            b = wsort[pl.ds(2 * lists[2 * most + j], 2)].reshape(2 * tile, cols)
            ps.append(jnp.dot(a, b, preferred_element_type=jnp.float32))
        for j, p in zip(js, ps):
            at = pl.ds(pl.multiple_of(lists[3 * most + j] * width, 8), width)
            acc[at, :] += p
        return _

    lax.fori_loop(0, lists[4 * most], group, 0)

    rows = acc.shape[0] // n_ck
    sub_row = lax.broadcasted_iota(jnp.int32, (SUB, cols), 0)
    for k in range(n_ck):
        at = jnp.bitwise_xor(mine, k) * rows
        if k == 0:
            own[...] = acc[pl.ds(pl.multiple_of(at, 8), rows), :]
            continue
        out = outs[k - 1]
        blocks = rows // SUB
        for b in range(blocks):
            if b % SUB == 0:
                scales = jnp.zeros((SUB, cols), jnp.float32)
            x = acc[pl.ds(pl.multiple_of(at + b * SUB, 8), SUB), :]
            top = jnp.max(jnp.max(jnp.abs(x), axis=1, keepdims=True), axis=0, keepdims=True)
            e = jnp.clip(jnp.ceil(jnp.log2(top) * 4.0), -400.0, 400.0)
            v = jnp.round(x * (jnp.exp2(e * -0.25) * QMAX)).astype(jnp.int32)
            out[b] = v.astype(jnp.int16)
            scales = jnp.where(sub_row == b % SUB, e, scales)
            if b % SUB == SUB - 1 or b == blocks - 1:
                out[blocks + b // SUB] = scales.astype(jnp.int32).astype(jnp.int16)


def contract(pieces, lists, wsort, n_ck):
    n_row = len(pieces)
    cap, width, tile = pieces[0].shape
    cols = wsort.shape[2]
    slots = n_row * cap
    rowt = wsort.shape[0] - slots
    rows = rowt * width // n_ck
    blocks = rows // SUB
    extra = -(-blocks // SUB)
    big = wsort.size * 2 > 24 << 20
    return pl.pallas_call(
        functools.partial(contract_kernel, n_row, n_ck),
        out_shape=[jax.ShapeDtypeStruct((rows, cols), jnp.float32)] + [jax.ShapeDtypeStruct((blocks + extra, SUB, cols), jnp.int16)] * (n_ck - 1),
        in_specs=[SMEM, VM] + [ANY] * n_row,
        out_specs=[VM] * n_ck,
        scratch_shapes=[
            pltpu.VMEM((slots + 1, width, tile), wsort.dtype),
            pltpu.VMEM((rowt * width, cols), jnp.float32),
            pltpu.SemaphoreType.DMA((n_row,)),
        ],
        cost_estimate=pl.CostEstimate(flops=2 * slots * width * tile * cols, bytes_accessed=slots * tile * cols * 2, transcendentals=0),
        compiler_params=pltpu.CompilerParams(vmem_limit_bytes=(56 << 20) if big else (20 << 20)),
        name="contract",
    )(lists, wsort, *pieces)


def finish_kernel(n_ck, units, row_gap, col_gap, *refs):
    parts, out = refs[:-1], refs[-1]
    n_row = out.shape[0]
    first = 0
    for c, n in enumerate(units):
        own, others = parts[c * n_ck], parts[c * n_ck + 1:(c + 1) * n_ck]
        blocks = n_row * n
        for b in range(blocks):
            x = own[pl.ds(b * SUB, SUB), :]
            for other in others:
                e = other[blocks + b // SUB].astype(jnp.int32).astype(jnp.float32)[b % SUB:b % SUB + 1, :]
                x += other[b].astype(jnp.int32).astype(jnp.float32) * (jnp.exp2(e * 0.25) * (1.0 / QMAX))
            r, i = b // n, first + b % n
            out[r, i] = (x / (row_gap[r, i] + col_gap[...])).astype(out.dtype)
        first += n


def finish(parts, row_gap, col_gap, n_ck, units):
    cols = col_gap.shape[-1]
    n_row, total = row_gap.shape[:2]
    return pl.pallas_call(
        functools.partial(finish_kernel, n_ck, units),
        out_shape=jax.ShapeDtypeStruct((n_row, total, SUB, cols), jnp.bfloat16),
        in_specs=[VM] * (2 + len(parts)),
        out_specs=VM,
        cost_estimate=pl.CostEstimate(flops=0, bytes_accessed=total * n_ck * n_row * SUB * cols * 4, transcendentals=0),
        compiler_params=pltpu.CompilerParams(vmem_limit_bytes=16 << 20),
        name="finish",
    )(row_gap, col_gap, *parts)


def shares(total):
    return SHARES if sum(SHARES) == total else (total,)


def on_device(amp_tiles, tile_pos, tile_count, cycle_integrals, row_gap, col_gap):
    n_row, n_ck = lax.axis_size("row"), lax.axis_size("ck")
    cap, tile = amp_tiles.shape[3], amp_tiles.shape[4]
    cols = cycle_integrals.shape[-1]
    run = row_gap.shape[0] // n_row
    units = shares(run // SUB)
    amp = amp_tiles.reshape(n_row, cap, tile // run, run // SUB, SUB, tile)
    w = cycle_integrals.reshape(-1, tile, cols)
    gap = row_gap.reshape(n_row, run // SUB, SUB, 1)
    lists, wsort = plan(tile_pos, tile_count, w, n_ck * n_row * run // tile)
    pieces, parts, first = [], [], 0

    def send(n, after):
        mine = pack(amp, first, n, after)
        return [mine[0]] + [lax.ppermute(mine[k], "row", [(i, i ^ k) for i in range(n_row)]) for k in range(1, n_row)]

    def multiply(piece):
        part = contract(piece, lists, wsort, n_ck)
        return [part[0]] + [lax.ppermute(part[k], "ck", [(i, i ^ k) for i in range(n_ck)]) for k in range(1, n_ck)]

    for c, n in enumerate(units):
        if c >= AHEAD:
            parts.append(multiply(pieces[c - AHEAD]))
        pieces.append(send(n, parts[-1][0] if parts else row_gap))
        first += n
    for piece in pieces[len(parts):]:
        parts.append(multiply(piece))
    parts = [x for part in parts for x in part]
    update = finish(parts, gap, col_gap.reshape(1, cols), n_ck, units)
    update = update.reshape(n_row * run, cols)
    return lax.all_to_all(update, "row", split_axis=0, concat_axis=0, tiled=True)


def solution(mesh):
    return jax.shard_map(
        on_device,
        mesh=mesh,
        in_specs=(
            P("row", "ck", None, None, None, None),
            P(None, "ck", None, None),
            P(None, "ck", None),
            P("ck", None),
            P(("row", "ck")),
            P(),
        ),
        out_specs=P(("row", "ck"), None),
        check_vma=False,
    )
```

```python
import functools
import jax
import jax.numpy as jnp
from jax import lax
from jax.experimental import pallas as pl
from jax.experimental.pallas import tpu as pltpu
from jax.sharding import PartitionSpec as P

LANE = 128
SUB = 8
UNROLL = 14
QMAX = 32000.0
LOTS = ((0, None, 24),)
SHARES = (2, 1, 1)
ANY = pl.BlockSpec(memory_space=pl.ANY)
HBM = pl.BlockSpec(memory_space=pltpu.HBM)
SMEM = pl.BlockSpec(memory_space=pltpu.SMEM)
VM = pl.BlockSpec(memory_space=pltpu.VMEM)


def pack_kernel(units, ks, amp, *refs):
    outs, (buf, sem_in, sem_out) = refs[:-3], refs[-3:]
    me = lax.axis_index("row")
    ins, puts = [], []
    for i, k in enumerate(ks):
        ins.append(pltpu.make_async_copy(amp.at[jnp.bitwise_xor(me, k)], buf.at[i], sem_in.at[i]))
        first = 0
        for c, n in enumerate(units):
            j = i * len(units) + c
            puts.append(pltpu.make_async_copy(buf.at[i, :, :, pl.ds(first, n)], outs[j], sem_out.at[j]))
            first += n
    for x in ins:
        x.start()
    for i, x in enumerate(ins):
        x.wait()
        for y in puts[i * len(units):(i + 1) * len(units)]:
            y.start()
    for y in puts:
        y.wait()


def pack(amp, units, ks, limit):
    _, cap, q, run, sub, tile = amp.shape
    outs = pl.pallas_call(
        functools.partial(pack_kernel, units, ks),
        out_shape=[jax.ShapeDtypeStruct((cap, q, n, sub, tile), amp.dtype) for _ in ks for n in units],
        in_specs=[HBM], out_specs=[VM] * (len(units) * len(ks)),
        scratch_shapes=[
            pltpu.VMEM((len(ks), cap, q, run, sub, tile), amp.dtype),
            pltpu.SemaphoreType.DMA((len(ks),)),
            pltpu.SemaphoreType.DMA((len(units) * len(ks),)),
        ],
        cost_estimate=pl.CostEstimate(flops=0, bytes_accessed=4 * amp.size, transcendentals=0),
        compiler_params=pltpu.CompilerParams(vmem_limit_bytes=limit << 20),
        name="pack",
    )(amp)
    return {(k, c): outs[i * len(units) + c].reshape(cap, -1, tile) for i, k in enumerate(ks) for c in range(len(units))}


def divider(kt, top):
    shift = 24
    mult = -(-(1 << shift) // kt)
    if top * mult < 1 << 31 and all((p * mult) >> shift == p // kt for p in range(top)):
        return lambda p: lax.shift_right_logical(p * mult, shift)
    return lambda p: p // kt


def plan_kernel(n_row, cap, kt, rowt, pos_in, cnt_in, w, lists, wbuf, seg, off, pos, cnt, table_sem, sem):
    me = lax.axis_index("row")
    slots = n_row * cap
    most = (lists.shape[0] - 1) // 3
    tile_of = divider(kt, kt * rowt)
    tables = [pltpu.make_async_copy(x, y, table_sem.at[i]) for i, (x, y) in enumerate([(pos_in, pos), (cnt_in, cnt)])]
    for x in tables:
        x.start()
    for x in tables:
        x.wait()
    for t in range(rowt):
        off[t] = t * (slots + 1)
    pltpu.make_async_copy(w.at[0], wbuf.at[slots], sem).start()

    def outer(k, total):
        s = jnp.bitwise_xor(me, k)
        n = cnt[s, 0, me]

        def inner(m, carry):
            p = pos[s, 0, me, m]
            t = tile_of(p)
            slot = k * cap + m
            pltpu.make_async_copy(w.at[p - t * kt], wbuf.at[slot], sem).start()
            i = off[t]
            seg[i] = slot
            off[t] = i + 1
            return carry

        lax.fori_loop(0, n, inner, 0)
        return total + n

    total = lax.fori_loop(0, n_row, outer, jnp.int32(1))
    at = jnp.int32(0)
    for t in range(rowt):
        base = t * (slots + 1)
        n = off[t] - base
        seg[base + n] = slots

        def pair(j, at):
            lists[at] = seg[base + 2 * j]
            lists[most + at] = seg[base + 2 * j + 1]
            lists[2 * most + at] = t
            return at + 1

        at = lax.fori_loop(0, (n + 1) // 2, pair, at)
    whole = (at + UNROLL - 1) // UNROLL

    def fill(j, carry):
        lists[j] = slots
        lists[most + j] = slots
        lists[2 * most + j] = 0
        return carry

    lax.fori_loop(at, whole * UNROLL, fill, 0)
    lists[3 * most] = whole

    def wait(i, carry):
        pltpu.make_async_copy(w.at[0], wbuf.at[slots], sem).wait()
        return carry

    lax.fori_loop(0, total, wait, 0)


def plan(pos, cnt, w, rowt):
    n_row, _, _, cap = pos.shape
    kt, tile, cols = w.shape
    slots = n_row * cap
    most = (slots + rowt) // 2 + UNROLL
    return pl.pallas_call(
        functools.partial(plan_kernel, n_row, cap, kt, rowt),
        out_shape=[jax.ShapeDtypeStruct((3 * most + 1,), jnp.int32), pltpu.VMEM((slots + 1, tile, cols), w.dtype)],
        in_specs=[HBM, HBM, HBM],
        out_specs=[SMEM, VM],
        scratch_shapes=[pltpu.SMEM((rowt * (slots + 1) + 1,), jnp.int32), pltpu.SMEM((rowt,), jnp.int32), pltpu.SMEM(pos.shape, jnp.int32), pltpu.SMEM(cnt.shape, jnp.int32), pltpu.SemaphoreType.DMA((2,)), pltpu.SemaphoreType.DMA],
        cost_estimate=pl.CostEstimate(flops=0, bytes_accessed=slots * tile * cols * 2, transcendentals=0),
        compiler_params=pltpu.CompilerParams(vmem_limit_bytes=4 << 20),
        name="plan",
    )(pltpu.with_memory_space_constraint(pos, pltpu.HBM), pltpu.with_memory_space_constraint(cnt, pltpu.HBM), w)


def contract_kernel(n_row, n_ck, lists, wbuf, *refs):
    pieces, own, outs = refs[:n_row], refs[n_row], refs[n_row + 1:n_row + n_ck]
    amp, acc = refs[n_row + n_ck:]
    mine = lax.axis_index("ck")
    cap, width, tile = pieces[0].shape
    slots = n_row * cap
    cols = acc.shape[1]
    most = (lists.shape[0] - 1) // 3
    acc[...] = jnp.zeros_like(acc)
    amp[slots] = jnp.zeros((width, tile), amp.dtype)
    for k in range(n_row):
        amp[pl.ds(k * cap, cap)] = pieces[k][...]

    def group(g, carry):
        js = [g * UNROLL + u for u in range(UNROLL)]
        ps = []
        for j in js:
            ids = lists[j], lists[most + j]
            a = jnp.concatenate([amp[i] for i in ids], axis=1)
            b = jnp.concatenate([wbuf[i] for i in ids], axis=0)
            ps.append(jnp.dot(a, b, preferred_element_type=jnp.float32))
        for j, p in zip(js, ps):
            at = pl.ds(pl.multiple_of(lists[2 * most + j] * width, 8), width)
            acc[at, :] += p
        return carry

    lax.fori_loop(0, lists[3 * most], group, 0)

    rows = acc.shape[0] // n_ck
    blocks, lanes = rows // SUB, cols // LANE
    sub_row = lax.broadcasted_iota(jnp.int32, (SUB, LANE), 0)
    for k in range(n_ck):
        at = jnp.bitwise_xor(mine, k) * rows
        if k == 0:
            own[...] = acc[pl.ds(pl.multiple_of(at, 8), rows), :]
            continue
        out = outs[k - 1]
        for b in range(blocks):
            if b % SUB == 0:
                scales = jnp.zeros((SUB, LANE), jnp.float32)
            x = acc[pl.ds(pl.multiple_of(at + b * SUB, 8), SUB), :]
            top = jnp.max(jnp.max(jnp.abs(x), axis=1, keepdims=True), axis=0, keepdims=True)
            e = jnp.clip(jnp.ceil(jnp.log2(top) * 4.0), -400.0, 400.0)
            v = jnp.round(x * (jnp.exp2(e * -0.25) * QMAX)).astype(jnp.int32).astype(jnp.int16)
            for i in range(lanes):
                out[b * lanes + i] = v[:, i * LANE:(i + 1) * LANE]
            scales = jnp.where(sub_row == b % SUB, e, scales)
            if b % SUB == SUB - 1 or b == blocks - 1:
                out[blocks * lanes + b // SUB] = scales.astype(jnp.int32).astype(jnp.int16)


def contract(pieces, lists, wbuf, n_ck, rowt):
    n_row = len(pieces)
    cap, width, tile = pieces[0].shape
    cols = wbuf.shape[2]
    slots = n_row * cap
    rows = rowt * width // n_ck
    blocks = rows // SUB
    extra = -(-blocks // SUB)
    big = wbuf.size * 2 > 24 << 20
    return pl.pallas_call(
        functools.partial(contract_kernel, n_row, n_ck),
        out_shape=[jax.ShapeDtypeStruct((rows, cols), jnp.float32)] + [jax.ShapeDtypeStruct((blocks * (cols // LANE) + extra, SUB, LANE), jnp.int16)] * (n_ck - 1),
        in_specs=[SMEM, VM] + [VM] * n_row,
        out_specs=[VM] * n_ck,
        scratch_shapes=[
            pltpu.VMEM((slots + 1, width, tile), wbuf.dtype),
            pltpu.VMEM((rowt * width, cols), jnp.float32),
        ],
        cost_estimate=pl.CostEstimate(flops=2 * slots * width * tile * cols, bytes_accessed=slots * tile * cols * 2, transcendentals=0),
        compiler_params=pltpu.CompilerParams(vmem_limit_bytes=(56 << 20) if big else (20 << 20)),
        name="contract",
    )(lists, wbuf, *pieces)


def finish_kernel(n_ck, units, row_gap, col_gap, *refs):
    parts, out = refs[:-1], refs[-1]
    n_row, cols = out.shape[0], out.shape[-1]
    lanes = cols // LANE
    first = 0
    for c, n in enumerate(units):
        own, others = parts[c * n_ck], parts[c * n_ck + 1:(c + 1) * n_ck]
        blocks = n_row * n
        for b in range(blocks):
            r, i = b // n, first + b % n
            factors = []
            for other in others:
                e = other[blocks * lanes + b // SUB].astype(jnp.int32).astype(jnp.float32)[b % SUB:b % SUB + 1, :]
                factors.append(jnp.exp2(e * 0.25) * (1.0 / QMAX))
            for l in range(lanes):
                at = pl.ds(l * LANE, LANE)
                x = own[pl.ds(b * SUB, SUB), at]
                for other, f in zip(others, factors):
                    x += other[b * lanes + l].astype(jnp.int32).astype(jnp.float32) * f
                out[r, i, :, at] = (x / (row_gap[r, i] + col_gap[:, at])).astype(out.dtype)
        first += n


def finish(parts, row_gap, col_gap, n_ck, units):
    cols = col_gap.shape[-1]
    n_row, total = row_gap.shape[:2]
    return pl.pallas_call(
        functools.partial(finish_kernel, n_ck, units),
        out_shape=jax.ShapeDtypeStruct((n_row, total, SUB, cols), jnp.bfloat16),
        in_specs=[VM] * (2 + len(parts)),
        out_specs=VM,
        cost_estimate=pl.CostEstimate(flops=0, bytes_accessed=total * n_ck * n_row * SUB * cols * 4, transcendentals=0),
        compiler_params=pltpu.CompilerParams(vmem_limit_bytes=16 << 20),
        name="finish",
    )(row_gap, col_gap, *parts)


def shares(total):
    return SHARES if sum(SHARES) == total else (total,)


def row_rank(k):
    return (k == 0, k == 1, k % 2, k)


def ck_rank(k):
    return -k


def on_device(amp_tiles, tile_pos, tile_count, cycle_integrals, row_gap, col_gap):
    n_row, n_ck = lax.axis_size("row"), lax.axis_size("ck")
    cap, tile = amp_tiles.shape[3], amp_tiles.shape[4]
    cols = cycle_integrals.shape[-1]
    run = row_gap.shape[0] // n_row
    units = shares(run // SUB)
    amp = pltpu.with_memory_space_constraint(amp_tiles.reshape(n_row, cap, tile // run, run // SUB, SUB, tile), pltpu.HBM)
    w = cycle_integrals.reshape(-1, tile, cols)
    gap = row_gap.reshape(n_row, run // SUB, SUB, 1)
    rowt = n_ck * n_row * run // tile
    lists, wbuf = plan(tile_pos, tile_count, w, rowt)
    pieces, parts = [], []
    order = sorted(range(n_row), key=row_rank)
    packed = {}
    for at, to, limit in LOTS:
        if order[at:to]:
            packed |= pack(amp, units, order[at:to], limit)
    for c in range(len(units)):
        mine = [packed[k, c] for k in range(n_row)]
        got = {k: lax.ppermute(mine[k], "row", [(i, i ^ k) for i in range(n_row)]) for k in sorted(range(1, n_row), key=row_rank)}
        pieces.append([mine[0]] + [got[k] for k in range(1, n_row)])
    for piece in pieces:
        part = contract(piece, lists, wbuf, n_ck, rowt)
        parts.append(part[0])
        got = {k: lax.ppermute(part[k], "ck", [(i, i ^ k) for i in range(n_ck)]) for k in sorted(range(1, n_ck), key=ck_rank)}
        parts += [got[k] for k in range(1, n_ck)]
    update = finish(parts, gap, col_gap.reshape(1, cols), n_ck, units)
    update = update.reshape(n_row * run, cols)
    return lax.all_to_all(update, "row", split_axis=0, concat_axis=0, tiled=True)


def solution(mesh):
    return jax.shard_map(
        on_device,
        mesh=mesh,
        in_specs=(
            P("row", "ck", None, None, None, None),
            P(None, "ck", None, None),
            P(None, "ck", None),
            P("ck", None),
            P(("row", "ck")),
            P(),
        ),
        out_specs=P(("row", "ck"), None),
        check_vma=False,
    )
```

```python
import functools
import jax
import jax.numpy as jnp
from jax import lax
from jax.experimental import pallas as pl
from jax.experimental.pallas import tpu as pltpu
from jax.sharding import PartitionSpec as P

LANE = 128
SUB = 8
UNROLL = 14
QMAX = 32000.0
LOTS = ((0, 3, 24), (3, None, 24))
SHARES = (2, 1, 1)
ANY = pl.BlockSpec(memory_space=pl.ANY)
HBM = pl.BlockSpec(memory_space=pltpu.HBM)
SMEM = pl.BlockSpec(memory_space=pltpu.SMEM)
VM = pl.BlockSpec(memory_space=pltpu.VMEM)


def pack_kernel(units, ks, amp, *refs):
    outs, (buf, sem_in, sem_out) = refs[:-3], refs[-3:]
    me = lax.axis_index("row")
    ins, puts = [], []
    for i, k in enumerate(ks):
        ins.append(pltpu.make_async_copy(amp.at[jnp.bitwise_xor(me, k)], buf.at[i], sem_in.at[i]))
        first = 0
        for c, n in enumerate(units):
            j = i * len(units) + c
            puts.append(pltpu.make_async_copy(buf.at[i, :, :, pl.ds(first, n)], outs[j], sem_out.at[j]))
            first += n
    for x in ins:
        x.start()
    for i, x in enumerate(ins):
        x.wait()
        for y in puts[i * len(units):(i + 1) * len(units)]:
            y.start()
    for y in puts:
        y.wait()


def pack(amp, units, ks, limit):
    _, cap, q, run, sub, tile = amp.shape
    outs = pl.pallas_call(
        functools.partial(pack_kernel, units, ks),
        out_shape=[jax.ShapeDtypeStruct((cap, q, n, sub, tile), amp.dtype) for _ in ks for n in units],
        in_specs=[HBM], out_specs=[VM] * (len(units) * len(ks)),
        scratch_shapes=[
            pltpu.VMEM((len(ks), cap, q, run, sub, tile), amp.dtype),
            pltpu.SemaphoreType.DMA((len(ks),)),
            pltpu.SemaphoreType.DMA((len(units) * len(ks),)),
        ],
        cost_estimate=pl.CostEstimate(flops=0, bytes_accessed=4 * amp.size, transcendentals=0),
        compiler_params=pltpu.CompilerParams(vmem_limit_bytes=limit << 20),
        name="pack",
    )(amp)
    return {(k, c): outs[i * len(units) + c].reshape(cap, -1, tile) for i, k in enumerate(ks) for c in range(len(units))}


def divider(kt, top):
    shift = 24
    mult = -(-(1 << shift) // kt)
    if top * mult < 1 << 31 and all((p * mult) >> shift == p // kt for p in range(top)):
        return lambda p: lax.shift_right_logical(p * mult, shift)
    return lambda p: p // kt


def plan_kernel(n_row, cap, kt, rowt, pos_in, cnt_in, w, lists, wbuf, seg, off, pos, cnt, table_sem, sem):
    me = lax.axis_index("row")
    slots = n_row * cap
    most = (lists.shape[0] - 1) // 3
    tile_of = divider(kt, kt * rowt)
    tables = [pltpu.make_async_copy(x, y, table_sem.at[i]) for i, (x, y) in enumerate([(pos_in, pos), (cnt_in, cnt)])]
    for x in tables:
        x.start()
    for x in tables:
        x.wait()
    for t in range(rowt):
        off[t] = t * (slots + 1)
    pltpu.make_async_copy(w.at[0], wbuf.at[slots], sem).start()

    def outer(k, total):
        s = jnp.bitwise_xor(me, k)
        n = cnt[s, 0, me]

        def inner(m, carry):
            p = pos[s, 0, me, m]
            t = tile_of(p)
            slot = k * cap + m
            pltpu.make_async_copy(w.at[p - t * kt], wbuf.at[slot], sem).start()
            i = off[t]
            seg[i] = slot
            off[t] = i + 1
            return carry

        lax.fori_loop(0, n, inner, 0)
        return total + n

    total = lax.fori_loop(0, n_row, outer, jnp.int32(1))
    at = jnp.int32(0)
    for t in range(rowt):
        base = t * (slots + 1)
        n = off[t] - base
        seg[base + n] = slots

        def pair(j, at):
            lists[at] = seg[base + 2 * j]
            lists[most + at] = seg[base + 2 * j + 1]
            lists[2 * most + at] = t
            return at + 1

        at = lax.fori_loop(0, (n + 1) // 2, pair, at)
    whole = (at + UNROLL - 1) // UNROLL

    def fill(j, carry):
        lists[j] = slots
        lists[most + j] = slots
        lists[2 * most + j] = 0
        return carry

    lax.fori_loop(at, whole * UNROLL, fill, 0)
    lists[3 * most] = whole

    def wait(i, carry):
        pltpu.make_async_copy(w.at[0], wbuf.at[slots], sem).wait()
        return carry

    lax.fori_loop(0, total, wait, 0)


def plan(pos, cnt, w, rowt):
    n_row, _, _, cap = pos.shape
    kt, tile, cols = w.shape
    slots = n_row * cap
    most = (slots + rowt) // 2 + UNROLL
    return pl.pallas_call(
        functools.partial(plan_kernel, n_row, cap, kt, rowt),
        out_shape=[jax.ShapeDtypeStruct((3 * most + 1,), jnp.int32), pltpu.VMEM((slots + 1, tile, cols), w.dtype)],
        in_specs=[HBM, HBM, HBM],
        out_specs=[SMEM, VM],
        scratch_shapes=[pltpu.SMEM((rowt * (slots + 1) + 1,), jnp.int32), pltpu.SMEM((rowt,), jnp.int32), pltpu.SMEM(pos.shape, jnp.int32), pltpu.SMEM(cnt.shape, jnp.int32), pltpu.SemaphoreType.DMA((2,)), pltpu.SemaphoreType.DMA],
        cost_estimate=pl.CostEstimate(flops=0, bytes_accessed=slots * tile * cols * 2, transcendentals=0),
        compiler_params=pltpu.CompilerParams(vmem_limit_bytes=4 << 20),
        name="plan",
    )(pltpu.with_memory_space_constraint(pos, pltpu.HBM), pltpu.with_memory_space_constraint(cnt, pltpu.HBM), w)


def contract_kernel(n_row, n_ck, lists, wbuf, *refs):
    pieces, own, outs = refs[:n_row], refs[n_row], refs[n_row + 1:n_row + n_ck]
    amp, acc = refs[n_row + n_ck:]
    mine = lax.axis_index("ck")
    cap, width, tile = pieces[0].shape
    slots = n_row * cap
    cols = acc.shape[1]
    most = (lists.shape[0] - 1) // 3
    acc[...] = jnp.zeros_like(acc)
    amp[slots] = jnp.zeros((width, tile), amp.dtype)
    for k in range(n_row):
        amp[pl.ds(k * cap, cap)] = pieces[k][...]

    def group(g, carry):
        js = [g * UNROLL + u for u in range(UNROLL)]
        ps = []
        for j in js:
            ids = lists[j], lists[most + j]
            a = jnp.concatenate([amp[i] for i in ids], axis=1)
            b = jnp.concatenate([wbuf[i] for i in ids], axis=0)
            ps.append(jnp.dot(a, b, preferred_element_type=jnp.float32))
        for j, p in zip(js, ps):
            at = pl.ds(pl.multiple_of(lists[2 * most + j] * width, 8), width)
            acc[at, :] += p
        return carry

    lax.fori_loop(0, lists[3 * most], group, 0)

    rows = acc.shape[0] // n_ck
    blocks, lanes = rows // SUB, cols // LANE
    sub_row = lax.broadcasted_iota(jnp.int32, (SUB, LANE), 0)
    for k in range(n_ck):
        at = jnp.bitwise_xor(mine, k) * rows
        if k == 0:
            own[...] = acc[pl.ds(pl.multiple_of(at, 8), rows), :]
            continue
        out = outs[k - 1]
        for b in range(blocks):
            if b % SUB == 0:
                scales = jnp.zeros((SUB, LANE), jnp.float32)
            x = acc[pl.ds(pl.multiple_of(at + b * SUB, 8), SUB), :]
            top = jnp.max(jnp.max(jnp.abs(x), axis=1, keepdims=True), axis=0, keepdims=True)
            e = jnp.clip(jnp.ceil(jnp.log2(top) * 4.0), -400.0, 400.0)
            v = jnp.round(x * (jnp.exp2(e * -0.25) * QMAX)).astype(jnp.int32).astype(jnp.int16)
            for i in range(lanes):
                out[b * lanes + i] = v[:, i * LANE:(i + 1) * LANE]
            scales = jnp.where(sub_row == b % SUB, e, scales)
            if b % SUB == SUB - 1 or b == blocks - 1:
                out[blocks * lanes + b // SUB] = scales.astype(jnp.int32).astype(jnp.int16)


def contract(pieces, lists, wbuf, n_ck, rowt):
    n_row = len(pieces)
    cap, width, tile = pieces[0].shape
    cols = wbuf.shape[2]
    slots = n_row * cap
    rows = rowt * width // n_ck
    blocks = rows // SUB
    extra = -(-blocks // SUB)
    big = wbuf.size * 2 > 24 << 20
    return pl.pallas_call(
        functools.partial(contract_kernel, n_row, n_ck),
        out_shape=[jax.ShapeDtypeStruct((rows, cols), jnp.float32)] + [jax.ShapeDtypeStruct((blocks * (cols // LANE) + extra, SUB, LANE), jnp.int16)] * (n_ck - 1),
        in_specs=[SMEM, VM] + [VM] * n_row,
        out_specs=[VM] * n_ck,
        scratch_shapes=[
            pltpu.VMEM((slots + 1, width, tile), wbuf.dtype),
            pltpu.VMEM((rowt * width, cols), jnp.float32),
        ],
        cost_estimate=pl.CostEstimate(flops=2 * slots * width * tile * cols, bytes_accessed=slots * tile * cols * 2, transcendentals=0),
        compiler_params=pltpu.CompilerParams(vmem_limit_bytes=(56 << 20) if big else (20 << 20)),
        name="contract",
    )(lists, wbuf, *pieces)


def finish_kernel(n_ck, units, row_gap, col_gap, *refs):
    parts, out = refs[:-1], refs[-1]
    n_row, cols = out.shape[0], out.shape[-1]
    lanes = cols // LANE
    first = 0
    for c, n in enumerate(units):
        own, others = parts[c * n_ck], parts[c * n_ck + 1:(c + 1) * n_ck]
        blocks = n_row * n
        for b in range(blocks):
            r, i = b // n, first + b % n
            factors = []
            for other in others:
                e = other[blocks * lanes + b // SUB].astype(jnp.int32).astype(jnp.float32)[b % SUB:b % SUB + 1, :]
                factors.append(jnp.exp2(e * 0.25) * (1.0 / QMAX))
            for l in range(lanes):
                at = pl.ds(l * LANE, LANE)
                x = own[pl.ds(b * SUB, SUB), at]
                for other, f in zip(others, factors):
                    x += other[b * lanes + l].astype(jnp.int32).astype(jnp.float32) * f
                out[r, i, :, at] = (x / (row_gap[r, i] + col_gap[:, at])).astype(out.dtype)
        first += n


def finish(parts, row_gap, col_gap, n_ck, units):
    cols = col_gap.shape[-1]
    n_row, total = row_gap.shape[:2]
    return pl.pallas_call(
        functools.partial(finish_kernel, n_ck, units),
        out_shape=jax.ShapeDtypeStruct((n_row, total, SUB, cols), jnp.bfloat16),
        in_specs=[VM] * (2 + len(parts)),
        out_specs=VM,
        cost_estimate=pl.CostEstimate(flops=0, bytes_accessed=total * n_ck * n_row * SUB * cols * 4, transcendentals=0),
        compiler_params=pltpu.CompilerParams(vmem_limit_bytes=16 << 20),
        name="finish",
    )(row_gap, col_gap, *parts)


def shares(total):
    return SHARES if sum(SHARES) == total else (total,)


def row_rank(k):
    return (k == 0, k == 1, k % 2, k)


def ck_rank(k):
    return k


def on_device(amp_tiles, tile_pos, tile_count, cycle_integrals, row_gap, col_gap):
    n_row, n_ck = lax.axis_size("row"), lax.axis_size("ck")
    cap, tile = amp_tiles.shape[3], amp_tiles.shape[4]
    cols = cycle_integrals.shape[-1]
    run = row_gap.shape[0] // n_row
    units = shares(run // SUB)
    amp = pltpu.with_memory_space_constraint(amp_tiles.reshape(n_row, cap, tile // run, run // SUB, SUB, tile), pltpu.HBM)
    w = cycle_integrals.reshape(-1, tile, cols)
    gap = row_gap.reshape(n_row, run // SUB, SUB, 1)
    rowt = n_ck * n_row * run // tile
    lists, wbuf = plan(tile_pos, tile_count, w, rowt)
    pieces, parts = [], []
    order = sorted(range(n_row), key=row_rank)
    packed = {}
    for at, to, limit in LOTS:
        if order[at:to]:
            packed |= pack(amp, units, order[at:to], limit)
    for c in range(len(units)):
        mine = [packed[k, c] for k in range(n_row)]
        got = {k: lax.ppermute(mine[k], "row", [(i, i ^ k) for i in range(n_row)]) for k in sorted(range(1, n_row), key=row_rank)}
        pieces.append([mine[0]] + [got[k] for k in range(1, n_row)])
    for piece in pieces:
        part = contract(piece, lists, wbuf, n_ck, rowt)
        parts.append(part[0])
        got = {k: lax.ppermute(part[k], "ck", [(i, i ^ k) for i in range(n_ck)]) for k in sorted(range(1, n_ck), key=ck_rank)}
        parts += [got[k] for k in range(1, n_ck)]
    update = finish(parts, gap, col_gap.reshape(1, cols), n_ck, units)
    update = update.reshape(n_row * run, cols)
    return lax.all_to_all(update, "row", split_axis=0, concat_axis=0, tiled=True)


def solution(mesh):
    return jax.shard_map(
        on_device,
        mesh=mesh,
        in_specs=(
            P("row", "ck", None, None, None, None),
            P(None, "ck", None, None),
            P(None, "ck", None),
            P("ck", None),
            P(("row", "ck")),
            P(),
        ),
        out_specs=P(("row", "ck"), None),
        check_vma=False,
    )
```
